32 devices in a mesh: rep: 16 (over z, y, x), head: 2 (over core).
Axes of the slice: x: 2, y: 2, z: 4, core: 2. Of those that a mesh axis runs over, the one named last changes fastest.
Arguments:
- queries: bfloat16 [2, 2048, 8192], P(None, 'rep', 'head'), may hold values from -200 to 200
- new_kv: bfloat16 [2, 2, 2048, 1024], P(None, None, 'rep', 'head'), may hold values from -8 to 8
- suffix_kv: bfloat16 [2, 2048, 32, 1024], P(None, 'rep', None, 'head'), may hold values from -8 to 8
- suffix_len: int32 [2048], P('rep'), may hold values from 2 to 32, as said below
- row_subtree: int32 [2048, 1], P('rep'), may hold values from 0 to 15, as said below
- owner_rep: int32 [16], replicated, may hold values from 0 to 15, each once
- prefix_kv: bfloat16 [16, 2, 1024, 1024], P('rep', None, None, 'head'), may hold values from -5 to 5
- out_weight: bfloat16 [8192, 4096], P('head'), may hold values from -0.25 to 0.25
Outputs:
- output: bfloat16 [2, 2048, 4096], P(None, 'rep', 'head')
The draws below stay inside these ranges and needn't reach their ends.
Inputs may be any that keep to these rules, and one draw needn't show every extreme that they name: `row_subtree`: at most 16 of one replica's 128 rows belong to one subtree; one subtree, drawn from the seed, has exactly 16 rows on every replica. `suffix_len`: every replica has rows with 32 live positions.
All inputs are finite; a program needn't handle non-finite values.
Results may differ from the reference program's by a relative error of at most 0.0053.
Values may be sent and summed in bfloat16 or wider, within the bound.
No kernel may reach another device: no remote copies, remote signals or barrier semaphores. Data moves between devices by JAX's collectives and lax.ppermute only.
A program may use at most 320 MiB of HBM per device.

```python
import math
import jax
import jax.numpy as jnp
from jax import lax

H = 64
KVH = 8
HD = 128
DOUT = 4096
P_SIZE = 1024
S = 32
ROWS_DEV = 128
SUB = 16
CAP = 16
ROWS = 2048


def noise_field(key_part, shape):
    return jnp.clip(jax.random.normal(key_part, shape, jnp.float32), -4.0, 4.0)


def spread_heads(kv_field):
    lead_dims = kv_field.shape[:-1]
    group_size = H // KVH
    shaped = kv_field.reshape(lead_dims + (KVH, 1, HD))
    return jnp.broadcast_to(shaped, lead_dims + (KVH, group_size, HD)).reshape(lead_dims + (H * HD,))


def joint_fields(key):
    base_key = jax.random.fold_in(key, 101)
    key_list = jax.random.split(base_key, 6)
    shared = jnp.clip(jax.random.normal(key_list[0], (ROWS, KVH * HD), jnp.float32), -4.0, 4.0)
    suffix_keys = noise_field(key_list[1], (ROWS, S, KVH * HD)) + 0.6 * shared[:, None, :]
    suffix_values = noise_field(key_list[2], (ROWS, S, KVH * HD))
    fresh_keys = noise_field(key_list[3], (2, ROWS, KVH * HD)) + 0.6 * shared[None]
    fresh_values = noise_field(key_list[4], (2, ROWS, KVH * HD))
    query_field = noise_field(key_list[5], (2, ROWS, H * HD)) + 0.6 * spread_heads(shared)[None] + 0.15 * spread_heads(fresh_keys)
    return (jnp.clip(query_field, -200.0, 200.0), suffix_keys, suffix_values, fresh_keys, fresh_values)


def draw_queries(key, part):
    return joint_fields(key)[0].astype(jnp.bfloat16)


def draw_new_kv(key, part):
    fields = joint_fields(key)
    return jnp.stack([fields[3], fields[4]]).astype(jnp.bfloat16)


def draw_suffix_kv(key, part):
    fields = joint_fields(key)
    return jnp.stack([fields[1], fields[2]]).astype(jnp.bfloat16)


def draw_suffix_len(key, part):
    lengths = jax.random.randint(jax.random.fold_in(key, 307), (ROWS,), 2, S + 1)
    return jnp.where(jnp.arange(ROWS) % 16 == 0, S, lengths).astype(jnp.int32)


def draw_row_subtree(key, part):
    hot_key = jax.random.fold_in(key, 211)
    hottest = jax.random.randint(hot_key, (), 0, SUB)
    others = (hottest + 1 + jnp.arange(SUB - 1)) % SUB
    pool_ids = jnp.repeat(others, CAP)

    def one_block(block_id):
        block_key = jax.random.fold_in(hot_key, block_id)
        first_key, second_key = jax.random.split(block_key)
        filler = jax.random.permutation(first_key, pool_ids)[:ROWS_DEV - CAP]
        merged = jnp.concatenate([jnp.full((CAP,), hottest, dtype=filler.dtype), filler])
        return jax.random.permutation(second_key, merged)
    blocks = jax.vmap(one_block)(jnp.arange(ROWS // ROWS_DEV))
    return blocks.reshape(ROWS, 1).astype(jnp.int32)


def block_levels(key, extent, cuts, low, top_value):
    factor_of = 1.0
    for dim, shards_of in cuts:
        steps = jax.random.uniform(jax.random.fold_in(jax.random.fold_in(key, 6), dim), (shards_of,), jnp.float32, low / len(cuts), top_value / len(cuts))
        factor_of = factor_of * jnp.repeat(jnp.exp(steps), extent[dim] // shards_of).reshape((-1,) + (1,) * (len(extent) - 1 - dim))
    return factor_of


def centred(rng, extent, scale, reach, cuts=(), kind=jnp.bfloat16):
    gain = block_levels(rng, extent, cuts, -0.22, 0.18) if cuts else 1.0
    entries = jax.random.normal(rng, extent, jnp.float32) * scale * gain
    return jnp.minimum(jnp.maximum(entries, -reach), reach).astype(kind)


def setup_inputs(seed: int = 0) -> dict:
    splits = jax.random.split(jax.random.key(seed), 9)
    return {
        "queries": draw_queries(jax.random.fold_in(splits[8], 71), 0),
        "new_kv": draw_new_kv(jax.random.fold_in(splits[8], 71), 0),
        "suffix_kv": draw_suffix_kv(jax.random.fold_in(splits[8], 71), 0),
        "suffix_len": draw_suffix_len(jax.random.fold_in(splits[8], 71), 0),
        "row_subtree": draw_row_subtree(jax.random.fold_in(splits[8], 71), 0),
        "owner_rep": jax.random.permutation(splits[5], SUB).astype(jnp.int32),
        "prefix_kv": centred(splits[6], (SUB, 2, P_SIZE, KVH * HD), 1.0, 5.0, ((0, 16), (3, 2))),
        "out_weight": centred(splits[7], (H * HD, DOUT), (4 * HD) ** -0.5, 0.25, ((0, 2),)),
    }


def prefix_part(query_rows, kv_block):
    kv_heads = kv_block.shape[-1] // HD
    count_rows = query_rows.shape[0]
    group_size = query_rows.shape[-1] // (kv_heads * HD)
    query_grid = query_rows.astype(jnp.float32).reshape(count_rows, 2, kv_heads, group_size, HD)
    key_grid = kv_block[0].astype(jnp.float32).reshape(-1, kv_heads, HD)
    value_grid = kv_block[1].astype(jnp.float32).reshape(-1, kv_heads, HD)
    scores = jnp.einsum('ctkgd,pkd->ctkgp', query_grid, key_grid) * (1.0 / math.sqrt(HD))
    highest = lax.optimization_barrier(jnp.max(scores, axis=-1))
    exp_terms = jnp.exp(scores - highest[..., None])
    totals = lax.optimization_barrier(jnp.sum(exp_terms, axis=-1))
    prob_round = lax.optimization_barrier(exp_terms.astype(jnp.bfloat16)).astype(jnp.float32)
    summed = jnp.einsum('ctkgp,pkd->ctkgd', prob_round, value_grid)
    part_out = (summed / totals[..., None]).astype(jnp.bfloat16).reshape(count_rows, 2, -1)
    part_lse = (highest + jnp.log(totals)).reshape(count_rows, 2, -1)
    return (part_out, part_lse)

def merge_suffix(query_rows, new_kv, suffix_kv, suffix_len, pre_out, pre_lse):
    row_count = query_rows.shape[0]
    kv_heads = suffix_kv.shape[-1] // HD
    group_size = query_rows.shape[-1] // (kv_heads * HD)
    cached = suffix_kv.shape[2]
    query_grid = query_rows.astype(jnp.float32).reshape(row_count, 2, kv_heads, group_size, HD)
    new_rows = jnp.transpose(new_kv, (0, 2, 1, 3))
    key_grid = jnp.concatenate([suffix_kv[0], new_rows[0]], axis=1).astype(jnp.float32).reshape(row_count, cached + 2, kv_heads, HD)
    value_grid = jnp.concatenate([suffix_kv[1], new_rows[1]], axis=1).astype(jnp.float32).reshape(row_count, cached + 2, kv_heads, HD)
    scores = jnp.einsum('rtkgd,rpkd->rtkgp', query_grid, key_grid) * (1.0 / math.sqrt(HD))
    position = jnp.arange(cached + 2, dtype=jnp.int32)[None, None, :]
    step_ids = jnp.arange(2, dtype=jnp.int32)[None, :, None]
    is_live = jnp.where(position < cached, position < suffix_len[:, None, None], position - cached <= step_ids)
    scores = jnp.where(is_live[:, :, None, None, :], scores, -jnp.inf)
    highest = lax.optimization_barrier(jnp.max(scores, axis=-1))
    exp_terms = jnp.exp(scores - highest[..., None])
    totals = lax.optimization_barrier(jnp.sum(exp_terms, axis=-1))
    prob_round = lax.optimization_barrier(exp_terms.astype(jnp.bfloat16)).astype(jnp.float32)
    summed = jnp.einsum('rtkgp,rpkd->rtkgd', prob_round, value_grid)
    prior_lse = pre_lse.reshape(row_count, 2, kv_heads, group_size)
    prior_out = pre_out.astype(jnp.float32).reshape(row_count, 2, kv_heads, group_size, HD)
    joint_top = jnp.maximum(prior_lse, highest)
    weight_pre = jnp.exp(prior_lse - joint_top)
    weight_suf = jnp.exp(highest - joint_top)
    mixed = (weight_pre[..., None] * prior_out + weight_suf[..., None] * summed) / (weight_pre + weight_suf * totals)[..., None]
    return mixed.astype(jnp.bfloat16).reshape(row_count, 2, -1)

def reference(queries, new_kv, suffix_kv, suffix_len, row_subtree, owner_rep, prefix_kv, out_weight):
    row_count = queries.shape[1]
    width_all = queries.shape[2]
    row_owner = owner_rep[row_subtree[:, 0]]
    most_rows = 2 * ROWS_DEV
    start_out = jnp.zeros((row_count, 2, width_all), jnp.bfloat16)
    start_lse = jnp.zeros((row_count, 2, H), jnp.float32)

    def visit_owner(state_pair, rep_id):
        slot_rows = jnp.nonzero(row_owner == rep_id, size=most_rows, fill_value=row_count)[0].astype(jnp.int32)
        safe_rows = jnp.minimum(slot_rows, row_count - 1).astype(jnp.int32)
        picked = jnp.transpose(jnp.take(queries, safe_rows, axis=1), (1, 0, 2))
        kv_block = lax.dynamic_index_in_dim(prefix_kv, rep_id, 0, keepdims=False)
        part_out, part_lse = prefix_part(picked, kv_block)
        return ((state_pair[0].at[slot_rows].set(part_out, mode='drop'), state_pair[1].at[slot_rows].set(part_lse, mode='drop')), None)
    (pre_out, pre_lse), unused = lax.scan(visit_owner, (start_out, start_lse), jnp.arange(SUB, dtype=jnp.int32))
    query_rows = jnp.transpose(queries, (1, 0, 2))
    attention = merge_suffix(query_rows, new_kv, suffix_kv, suffix_len, pre_out, pre_lse)
    attn_steps = jnp.transpose(attention, (1, 0, 2)).reshape(2 * row_count, -1)
    projected = jnp.dot(attn_steps, out_weight, preferred_element_type=jnp.float32)
    return projected.astype(jnp.bfloat16).reshape(2, row_count, -1)
```

```python
import functools
import math

import jax
import jax.numpy as jnp
from jax import lax
from jax.experimental import pallas as pl
from jax.experimental.pallas import tpu as pltpu
from jax.sharding import PartitionSpec as P

HD = 128
PLANE = 4
CHUNKS = 2
SCALE = 1.0 / math.sqrt(HD)
EXP2_SCALE = SCALE * math.log2(math.e)
NEG = -1e30
VMEM_LIMIT = 60 << 20


def params(steps):
    return pltpu.CompilerParams(
        dimension_semantics=("arbitrary",) * steps, vmem_limit_bytes=VMEM_LIMIT
    )


def dot_nt(a, b):
    return lax.dot_general(a, b, (((1,), (1,)), ((), ())), preferred_element_type=jnp.float32)


def place_queries(slot_row, queries, chunk, chunks):
    steps, rows, width = queries.shape
    kv_heads = width // (8 * HD)
    per = kv_heads // chunks
    cap = 16
    pairs = steps * 8

    def body(slot_ref, q_ref, *outs):
        slots = PLANE * 4 * cap
        onehot = (
            lax.broadcasted_iota(jnp.int32, (slots, rows), 0) == slot_ref[...]
        ).astype(jnp.bfloat16)
        for t in range(steps):
            for g2 in range(4):
                y = jnp.dot(
                    onehot,
                    q_ref[t, :, g2 * 2 * HD : (g2 + 1) * 2 * HD],
                    preferred_element_type=jnp.float32,
                ).astype(jnp.bfloat16)
                for half in range(2):
                    tg = t * 8 + g2 * 2 + half
                    for m in range(PLANE):
                        for s in range(4):
                            base = (m * 4 + s) * cap
                            outs[m][0, s, tg * cap : (tg + 1) * cap, :] = y[
                                base : base + cap, half * HD : (half + 1) * HD
                            ]

    out = jax.ShapeDtypeStruct((per, 4, pairs * cap, HD), jnp.bfloat16)
    return pl.pallas_call(
        body,
        grid=(per,),
        in_specs=[
            pl.BlockSpec((1, rows), lambda k: (0, 0)),
            pl.BlockSpec((steps, rows, 8 * HD), lambda k: (0, 0, chunk * per + k)),
        ],
        out_specs=[pl.BlockSpec((1, 4, pairs * cap, HD), lambda k: (k, 0, 0, 0))] * PLANE,
        out_shape=[out] * PLANE,
        compiler_params=params(1),
        cost_estimate=pl.CostEstimate(
            flops=per * 2 * 256 * rows * 16 * HD, bytes_accessed=per * 3 << 19, transcendentals=0
        ),
        name="place_queries",
    )(slot_row, queries)


def prefix_tile(q, keys, values):
    rows = q.shape[0]
    cap = 16
    scores = dot_nt(q, keys)
    highest = jnp.max(scores, axis=-1, keepdims=True)
    exp_terms = jnp.exp2((scores - highest) * EXP2_SCALE)
    totals = jnp.sum(exp_terms, axis=-1, keepdims=True)
    summed = jnp.dot(exp_terms.astype(jnp.bfloat16), values, preferred_element_type=jnp.float32)
    part = (summed / totals).astype(jnp.bfloat16)
    lse = (highest * SCALE + jnp.log(totals)).reshape(rows // cap, cap, 1)
    lane = lax.broadcasted_iota(jnp.int32, (cap, HD), 1)
    packed = jnp.zeros((cap, HD), jnp.float32)
    for tg in range(rows // cap):
        packed = jnp.where((lane & 15) == tg, lse[tg], packed)
    hi = packed.astype(jnp.bfloat16)
    rest = packed - hi.astype(jnp.float32)
    mid = rest.astype(jnp.bfloat16)
    low = (rest - mid.astype(jnp.float32)).astype(jnp.bfloat16)
    part_lse = jnp.where(lane < 16, hi, jnp.where(lane < 32, mid, low))
    return part, part_lse


def prefix_call(inner, sources, kvs, jobs, out_subs, name):
    per = sources[0][0].shape[0]
    unit = sources[0][0].shape[2]
    cap = 16
    flat = [a for group in sources for a in group]
    n_src, n_kv = len(flat), len(kvs)
    length = kvs[0].shape[1]

    def body(inner_ref, *refs):
        src = refs[:n_src]
        kv = refs[n_src : n_src + n_kv]
        outs = refs[n_src + n_kv : -2]
        q_scr, o_scr = refs[-2:]
        job_id = pl.program_id(1)
        is_inner = inner_ref[0] == 1
        for ji, (si, sub, ki, oi, osub, only_inner) in enumerate(jobs):
            run = job_id == ji
            if only_inner:
                run = jnp.logical_and(run, is_inner)

                @pl.when(jnp.logical_and(job_id == ji, jnp.logical_not(is_inner)))
                def _(oi=oi, osub=osub):
                    for m in range(PLANE):
                        outs[oi * PLANE + m][0, osub] = jnp.zeros((unit + cap, HD), jnp.bfloat16)

            @pl.when(run)
            def _(si=si, sub=sub, ki=ki, oi=oi, osub=osub):
                for m in range(PLANE):
                    q_scr[m] = src[si * PLANE + m][0, sub]

                def step(m, carry):
                    part, part_lse = prefix_tile(q_scr[m], kv[ki][0], kv[ki][1])
                    o_scr[m, :unit] = part
                    o_scr[m, unit:] = part_lse
                    return carry

                lax.fori_loop(0, PLANE, step, 0)
                for m in range(PLANE):
                    outs[oi * PLANE + m][0, osub] = o_scr[m]

    out_shape, out_specs = [], []
    for subs in out_subs:
        for m in range(PLANE):
            out_shape.append(jax.ShapeDtypeStruct((per, subs, unit + cap, HD), jnp.bfloat16))
            out_specs.append(
                pl.BlockSpec((1, subs, unit + cap, HD), lambda k, j, inner: (k, 0, 0, 0))
            )
    work = per * len(jobs) * PLANE * unit * length
    outs = pl.pallas_call(
        body,
        grid_spec=pltpu.PrefetchScalarGridSpec(
            num_scalar_prefetch=1,
            grid=(per, len(jobs)),
            in_specs=[
                pl.BlockSpec((1,) + a.shape[1:], lambda k, j, inner: (k, 0, 0, 0)) for a in flat
            ]
            + [pl.BlockSpec((2, length, HD), lambda k, j, inner: (0, 0, k)) for _ in kvs],
            out_specs=out_specs,
            scratch_shapes=[
                pltpu.VMEM((PLANE, unit, HD), jnp.bfloat16),
                pltpu.VMEM((PLANE, unit + cap, HD), jnp.bfloat16),
            ],
        ),
        out_shape=out_shape,
        compiler_params=params(2),
        cost_estimate=pl.CostEstimate(
            flops=work * 4 * HD * 2, bytes_accessed=per * 4 << 20, transcendentals=work
        ),
        name=name,
    )(inner, *flat, *kvs)
    return [list(outs[i * PLANE : (i + 1) * PLANE]) for i in range(len(out_subs))]


def suffix_call(queries, new_kv, suffix_kv, key_row):
    steps, rows, width = queries.shape
    kv_heads = width // (8 * HD)
    cached = suffix_kv.shape[2]
    rb = 16
    pairs = steps * 8
    keys_n = rb * cached

    def body(q_ref, new_ref, kv_ref, live_ref, acc_ref, stat_ref):
        q = jnp.concatenate(
            [q_ref[t, :, g * HD : (g + 1) * HD] for t in range(steps) for g in range(8)], axis=0
        )
        scores = dot_nt(q, kv_ref[0].reshape(keys_n, HD))
        fresh = dot_nt(q, new_ref[0].reshape(steps * rb, HD))
        row_id = lax.broadcasted_iota(jnp.int32, scores.shape, 0) & (rb - 1)
        scores = jnp.where(row_id == live_ref[0], scores, NEG)
        qi = lax.broadcasted_iota(jnp.int32, fresh.shape, 0)
        ki = lax.broadcasted_iota(jnp.int32, fresh.shape, 1)
        same = (qi & (rb - 1)) == (ki & (rb - 1))
        seen = lax.div(ki, rb) <= lax.div(qi, 8 * rb)
        fresh = jnp.where(jnp.logical_and(same, seen), fresh, NEG)
        highest = jnp.maximum(
            jnp.max(scores, axis=-1, keepdims=True), jnp.max(fresh, axis=-1, keepdims=True)
        )
        exp_terms = jnp.exp2((scores - highest) * EXP2_SCALE)
        exp_fresh = jnp.exp2((fresh - highest) * EXP2_SCALE)
        totals = jnp.sum(exp_terms, axis=-1, keepdims=True) + jnp.sum(
            exp_fresh, axis=-1, keepdims=True
        )
        acc = jnp.dot(
            exp_terms.astype(jnp.bfloat16),
            kv_ref[1].reshape(keys_n, HD),
            preferred_element_type=jnp.float32,
        ) + jnp.dot(
            exp_fresh.astype(jnp.bfloat16),
            new_ref[1].reshape(steps * rb, HD),
            preferred_element_type=jnp.float32,
        )
        acc_ref[0] = acc.reshape(pairs, rb, HD)
        top = (highest * SCALE).reshape(pairs, rb, 1)
        totals = totals.reshape(pairs, rb, 1)
        lane = lax.broadcasted_iota(jnp.int32, (rb, HD), 1)
        stat = jnp.ones((rb, HD), jnp.float32)
        for tg in range(pairs):
            stat = jnp.where(lane == tg, top[tg], stat)
            stat = jnp.where(lane == pairs + tg, totals[tg], stat)
        stat_ref[0] = stat

    return pl.pallas_call(
        body,
        grid=(kv_heads, rows // rb),
        in_specs=[
            pl.BlockSpec((steps, rb, 8 * HD), lambda k, r: (0, r, k)),
            pl.BlockSpec((2, steps, rb, HD), lambda k, r: (0, 0, r, k)),
            pl.BlockSpec((2, rb, cached, HD), lambda k, r: (0, r, 0, k)),
            pl.BlockSpec((1, 1, keys_n), lambda k, r: (r, 0, 0)),
        ],
        out_specs=[
            pl.BlockSpec((1, pairs, rb, HD), lambda k, r: (k, 0, r, 0)),
            pl.BlockSpec((1, rb, HD), lambda k, r: (k, r, 0)),
        ],
        out_shape=[
            jax.ShapeDtypeStruct((kv_heads, pairs, rows, HD), jnp.float32),
            jax.ShapeDtypeStruct((kv_heads, rows, HD), jnp.float32),
        ],
        compiler_params=params(2),
        cost_estimate=pl.CostEstimate(
            flops=kv_heads * 8 * 256 * 512 * 512 * 2,
            bytes_accessed=16 << 20,
            transcendentals=kv_heads * 8 * 256 * 512,
        ),
        name="suffix_attention",
    )(queries, new_kv, suffix_kv, key_row)


def merge_call(spots, parts, suf_acc, suf_stat, chunk):
    per = parts[0].shape[0]
    unit = parts[0].shape[2] - 16
    cap = 16
    pairs = unit // cap
    rows = suf_acc.shape[2]
    places = [(i, s) for i, a in enumerate(parts) for s in range(a.shape[1])]
    total = len(places) * cap
    n = len(parts)

    def body(spot_ref, *refs):
        part = refs[:n]
        acc_ref, stat_ref, out_ref = refs[n:]
        onehot = (
            lax.broadcasted_iota(jnp.int32, (rows, total), 1) == spot_ref[...]
        ).astype(jnp.bfloat16)

        def pick(lo):
            block = jnp.concatenate([part[i][0, s, lo : lo + cap, :] for i, s in places], axis=0)
            return jnp.dot(onehot, block, preferred_element_type=jnp.float32)

        lse = pick(unit)
        lse = lse + pltpu.roll(lse, HD - 16, 1) + pltpu.roll(lse, HD - 32, 1)
        top = stat_ref[0]
        totals = pltpu.roll(top, HD - pairs, 1)
        joint = jnp.maximum(lse, top)
        pre = jnp.exp(lse - joint)
        suf = jnp.exp(top - joint)
        norm = pre + suf * totals
        pre = pre / norm
        suf = suf / norm
        for tg in range(pairs):
            t, g = tg // 8, tg % 8
            mixed = pre[:, tg : tg + 1] * pick(tg * cap) + suf[:, tg : tg + 1] * acc_ref[0, tg]
            out_ref[t * rows : (t + 1) * rows, g * HD : (g + 1) * HD] = mixed.astype(jnp.bfloat16)

    return pl.pallas_call(
        body,
        grid=(per,),
        in_specs=[pl.BlockSpec((rows, 1), lambda k: (0, 0))]
        + [pl.BlockSpec((1,) + a.shape[1:], lambda k: (k, 0, 0, 0)) for a in parts]
        + [
            pl.BlockSpec((1, pairs, rows, HD), lambda k: (chunk * per + k, 0, 0, 0)),
            pl.BlockSpec((1, rows, HD), lambda k: (chunk * per + k, 0, 0)),
        ],
        out_specs=pl.BlockSpec((2 * rows, 8 * HD), lambda k: (0, k)),
        out_shape=jax.ShapeDtypeStruct((2 * rows, per * 8 * HD), jnp.bfloat16),
        compiler_params=params(1),
        cost_estimate=pl.CostEstimate(
            flops=per * 17 * 2 * rows * total * HD, bytes_accessed=per * 4 << 20, transcendentals=0
        ),
        name="merge_parts",
    )(spots, *parts, suf_acc, suf_stat)


def project_call(half, attn, weight, prior, chunk, cols, name):
    rows, depth = attn.shape
    tile = 512
    steps = cols // tile

    def body(half_ref, attn_ref, w_ref, *refs):
        out = jnp.dot(attn_ref[...], w_ref[...], preferred_element_type=jnp.float32)
        if prior is not None:
            out = out + refs[0][...]
        refs[-1][...] = out

    in_specs = [
        pl.BlockSpec((rows, depth), lambda n, half: (0, 0)),
        pl.BlockSpec((depth, tile), lambda n, half: (chunk, half[0] * steps + n)),
    ]
    args = [attn, weight]
    if prior is not None:
        in_specs.append(pl.BlockSpec((rows, tile), lambda n, half: (0, half[0] * steps + n)))
        args.append(prior)
    return pl.pallas_call(
        body,
        grid_spec=pltpu.PrefetchScalarGridSpec(
            num_scalar_prefetch=1,
            grid=(steps,),
            in_specs=in_specs,
            out_specs=pl.BlockSpec((rows, tile), lambda n, half: (0, n)),
        ),
        out_shape=jax.ShapeDtypeStruct((rows, cols), jnp.float32),
        compiler_params=params(1),
        cost_estimate=pl.CostEstimate(
            flops=2 * rows * depth * cols,
            bytes_accessed=2 * depth * cols + 8 * rows * cols,
            transcendentals=0,
        ),
        name=name,
    )(half, *args)


def attend(query_slots, kv_blocks):
    count_n = query_slots.shape[0]
    count_c = query_slots.shape[1]
    kv_heads = kv_blocks.shape[-1] // HD
    group_size = query_slots.shape[-1] // (kv_heads * HD)
    query_grid = query_slots.reshape(count_n, count_c, 2, kv_heads, group_size, HD)
    key_grid = kv_blocks[:, 0].reshape(count_n, -1, kv_heads, HD)
    value_grid = kv_blocks[:, 1].reshape(count_n, -1, kv_heads, HD)
    scores = jnp.einsum(
        "nctkgd,npkd->nctkgp", query_grid, key_grid, preferred_element_type=jnp.float32
    ) * (1.0 / math.sqrt(HD))
    highest = jnp.max(scores, axis=-1)
    exp_terms = jnp.exp(scores - highest[..., None])
    totals = jnp.sum(exp_terms, axis=-1)
    prob_round = exp_terms.astype(jnp.bfloat16)
    summed = jnp.einsum(
        "nctkgp,npkd->nctkgd", prob_round, value_grid, preferred_element_type=jnp.float32
    )
    part_out = (summed / totals[..., None]).astype(jnp.bfloat16).reshape(count_n, count_c, 2, -1)
    part_lse = (highest + jnp.log(totals)).reshape(count_n, count_c, 2, -1)
    return (part_out, part_lse)


def merge_suffix(queries, new_kv, suffix_kv, suffix_len, pre_out, pre_lse):
    local_rows = queries.shape[1]
    kv_heads = suffix_kv.shape[-1] // HD
    group_size = queries.shape[-1] // (kv_heads * HD)
    cached = suffix_kv.shape[2]
    query_grid = jnp.transpose(queries, (1, 0, 2)).reshape(local_rows, 2, kv_heads, group_size, HD)
    new_rows = jnp.transpose(new_kv, (0, 2, 1, 3))
    key_grid = jnp.concatenate([suffix_kv[0], new_rows[0]], axis=1).reshape(
        local_rows, cached + 2, kv_heads, HD
    )
    value_grid = jnp.concatenate([suffix_kv[1], new_rows[1]], axis=1).reshape(
        local_rows, cached + 2, kv_heads, HD
    )
    scores = jnp.einsum(
        "rtkgd,rpkd->rtkgp", query_grid, key_grid, preferred_element_type=jnp.float32
    ) * (1.0 / math.sqrt(HD))
    position = jnp.arange(cached + 2, dtype=jnp.int32)[None, None, :]
    step_ids = jnp.arange(2, dtype=jnp.int32)[None, :, None]
    is_live = jnp.where(
        position < cached, position < suffix_len[:, None, None], position - cached <= step_ids
    )
    scores = jnp.where(is_live[:, :, None, None, :], scores, -jnp.inf)
    highest = jnp.max(scores, axis=-1)
    exp_terms = jnp.exp(scores - highest[..., None])
    totals = jnp.sum(exp_terms, axis=-1)
    prob_round = exp_terms.astype(jnp.bfloat16)
    summed = jnp.einsum(
        "rtkgp,rpkd->rtkgd", prob_round, value_grid, preferred_element_type=jnp.float32
    )
    prior_lse = pre_lse.reshape(local_rows, 2, kv_heads, group_size)
    prior_out = pre_out.astype(jnp.float32).reshape(local_rows, 2, kv_heads, group_size, HD)
    joint_top = jnp.maximum(prior_lse, highest)
    weight_pre = jnp.exp(prior_lse - joint_top)
    weight_suf = jnp.exp(highest - joint_top)
    mixed = (weight_pre[..., None] * prior_out + weight_suf[..., None] * summed) / (
        weight_pre + weight_suf * totals
    )[..., None]
    return mixed.astype(jnp.bfloat16).reshape(local_rows, 2, -1)


def gathered_device(
    queries, new_kv, suffix_kv, suffix_len, row_subtree, owner_rep, prefix_kv, out_weight
):
    local_rows = queries.shape[1]
    replicas = lax.axis_size("rep")
    capacity = 2 * local_rows // replicas
    subtrees = owner_rep.shape[0]
    sub_table = (row_subtree == jnp.arange(subtrees, dtype=jnp.int32)[None, :]).astype(jnp.int32)
    row_owner = jnp.sum(sub_table * owner_rep[None, :], axis=1)
    own_table = (row_owner[:, None] == jnp.arange(subtrees, dtype=jnp.int32)[None, :]).astype(
        jnp.int32
    )
    earlier = jnp.cumsum(own_table, axis=0) - own_table
    slot_index = row_owner * capacity + jnp.sum(earlier * own_table, axis=1)
    placing = (
        slot_index[None, :] == jnp.arange(subtrees * capacity, dtype=jnp.int32)[:, None]
    ).astype(jnp.bfloat16)
    query_slots = jnp.einsum(
        "sr,trx->stx", placing, queries, preferred_element_type=jnp.float32
    ).astype(jnp.bfloat16)
    query_slots = query_slots.reshape(subtrees, capacity, 2, -1)
    part_out, part_lse = attend(query_slots, lax.all_gather(prefix_kv, "rep", axis=0, tiled=True))
    pre_out = jnp.take(part_out.reshape(subtrees * capacity, 2, -1), slot_index, axis=0)
    pre_lse = jnp.take(part_lse.reshape(subtrees * capacity, 2, -1), slot_index, axis=0)
    attention = merge_suffix(queries, new_kv, suffix_kv, suffix_len, pre_out, pre_lse)
    attn_steps = jnp.transpose(attention, (1, 0, 2)).reshape(2 * local_rows, -1)
    head_terms = jnp.dot(attn_steps, out_weight, preferred_element_type=jnp.float32).reshape(
        2, local_rows, -1
    )
    return lax.psum_scatter(head_terms, "head", scatter_dimension=2, tiled=True).astype(
        jnp.bfloat16
    )


def routed_device(
    queries, new_kv, suffix_kv, suffix_len, row_subtree, owner_rep, prefix_kv, out_weight
):
    rows = queries.shape[1]
    replicas = lax.axis_size("rep")
    levels = replicas // PLANE
    me = lax.axis_index("rep")
    head = lax.axis_index("head")
    level, seat = me // PLANE, me % PLANE
    kv_heads = suffix_kv.shape[-1] // HD
    per = kv_heads // CHUNKS
    cached = suffix_kv.shape[2]
    cap = 16

    def perm(move):
        pairs = []
        for r in range(replicas):
            to = move(r // PLANE, r % PLANE)
            if to is not None:
                pairs.append((r, to[0] * PLANE + to[1]))
        return pairs

    def is_end(v):
        return v in (0, levels - 1)

    def send(a, move):
        return lax.ppermute(a, "rep", perm(move))

    def beside(m):
        return lambda v, s: (v, s ^ m)

    def to_pair(v, s):
        return (v ^ 1, s)

    def across(v, s):
        return None if is_end(v) else (levels - 1 - v, s)

    def inward(v, s):
        return (v ^ 1, s) if is_end(v) else None

    def outward(m):
        return lambda v, s: None if is_end(v) else (v ^ 1, s ^ m)

    own, pair, mid, far = [], [], [], []
    for c in range(CHUNKS):
        kv = prefix_kv[0, :, :, c * per * HD : (c + 1) * per * HD]
        own.append(kv)
        pair.append(send(kv, to_pair))
        mid.append(send(kv, across))

    sub_table = row_subtree == jnp.arange(owner_rep.shape[0], dtype=jnp.int32)[None, :]
    owner = jnp.sum(jnp.where(sub_table, owner_rep[None, :], 0), axis=1)
    ids = jnp.arange(rows, dtype=jnp.int32)
    rank = jnp.sum(
        jnp.logical_and(owner[:, None] == owner[None, :], ids[None, :] < ids[:, None]).astype(
            jnp.int32
        ),
        axis=1,
    )
    owner_level, owner_seat = owner // PLANE, owner % PLANE
    partner = owner_seat ^ seat
    end_level = jnp.logical_or(owner_level == 0, owner_level == levels - 1)
    kind = jnp.where(
        owner_level == level,
        0,
        jnp.where(owner_level == (level ^ 1), 1, jnp.where(end_level, 3, 2)),
    )
    slot = (partner * 4 + kind) * cap + rank
    inner = jnp.logical_not(jnp.logical_or(level == 0, level == levels - 1))
    from_inner = PLANE * 3 * cap + PLANE * cap + (partner * 2 + kind - 2) * cap + rank
    local = jnp.where(
        kind < 3, (partner * 3 + kind) * cap + rank, PLANE * 3 * cap + partner * cap + rank
    )
    spots = jnp.where(jnp.logical_or(kind < 2, inner), local, from_inner)[:, None]
    inner_flag = inner.astype(jnp.int32)[None]
    position = jnp.arange(cached, dtype=jnp.int32)[None, :]
    key_row = jnp.where(position < suffix_len[:, None], (ids & 15)[:, None], -1).reshape(
        rows // 16, 1, 16 * cached
    )

    asked, asked_ends = [], []
    for c in range(CHUNKS):
        mine = place_queries(slot[None, :], queries, c, CHUNKS)
        got = [mine[0]] + [send(mine[m], beside(m)) for m in range(1, PLANE)]
        asked.append(got)
        asked_ends.append(send(jnp.stack([g[:, 2:] for g in got]), inward))
    for c in range(CHUNKS):
        far.append(send(pair[c], across))

    suf_acc, suf_stat = suffix_call(queries, new_kv, suffix_kv, key_row)

    near, last, ends = [], [], []
    for c in range(CHUNKS):
        (o,) = prefix_call(
            inner_flag,
            [asked[c]],
            [own[c], pair[c], mid[c]],
            [(0, 0, 0, 0, 0, False), (0, 1, 1, 0, 1, False), (0, 2, 2, 0, 2, True)],
            [3],
            "prefix_near",
        )
        near.append([o[0]] + [send(o[m], beside(m)) for m in range(1, PLANE)])
        e = [asked_ends[c][m] for m in range(PLANE)]
        oe, od = prefix_call(
            inner_flag,
            [asked[c], e],
            [mid[c], far[c]],
            [
                (1, 0, 0, 0, 0, True),
                (1, 1, 1, 0, 1, True),
                (0, 3, 1, 1, 0, True),
            ],
            [2, 1],
            "prefix_far",
        )
        ends.append([send(oe[m], outward(m)) for m in range(PLANE)])
        last.append([od[0]] + [send(od[m], beside(m)) for m in range(1, PLANE)])

    total = None
    zero = jnp.zeros((1,), jnp.int32)
    for c in range(CHUNKS):
        attn = merge_call(spots, near[c] + last[c] + ends[c], suf_acc, suf_stat, c)
        if c < CHUNKS - 1:
            total = project_call(
                zero, attn, out_weight, total, c, out_weight.shape[1], "project_all"
            )
    half = out_weight.shape[1] // 2
    theirs = project_call(
        (1 - head).astype(jnp.int32)[None], attn, out_weight, total, c, half, "project_theirs"
    )
    theirs = lax.ppermute(theirs, "head", [(0, 1), (1, 0)])
    ours = project_call(
        head.astype(jnp.int32)[None], attn, out_weight, total, c, half, "project_ours"
    )
    return (ours + theirs).astype(jnp.bfloat16).reshape(2, rows, half)


def solution(mesh):
    placed = (
        P(None, "rep", "head"),
        P(None, None, "rep", "head"),
        P(None, "rep", None, "head"),
        P("rep"),
        P("rep", None),
        P(),
        P("rep", None, None, "head"),
        P("head", None),
    )
    line_of_four = mesh.shape["rep"] == 4 * PLANE and mesh.shape["head"] == 2
    return jax.shard_map(
        routed_device if line_of_four else gathered_device,
        mesh=mesh,
        in_specs=placed,
        out_specs=P(None, "rep", "head"),
        check_vma=False,
    )
```

```python
import functools
import math

import jax
import jax.numpy as jnp
from jax import lax
from jax.experimental import pallas as pl
from jax.experimental.pallas import tpu as pltpu
from jax.sharding import PartitionSpec as P


HD = 128
PLANE = 4
SPLIT = (0.5, 0.5)
SCALE = 1.0 / math.sqrt(HD)
EXP2_SCALE = SCALE * math.log2(math.e)
NEG = -1e30
VMEM_WHOLE = 60 << 20
VMEM_PART = 28 << 20


def params(steps, limit=VMEM_WHOLE):
    return pltpu.CompilerParams(
        dimension_semantics=("arbitrary",) * steps, vmem_limit_bytes=limit
    )


def dot_nt(a, b):
    return lax.dot_general(a, b, (((1,), (1,)), ((), ())), preferred_element_type=jnp.float32)


def place_queries(slot_row, queries, first, per):
    steps, rows = queries.shape[:2]
    cap = 16
    pairs = steps * 8

    def body(slot_ref, q_ref, *outs):
        slots = PLANE * 4 * cap
        onehot = (
            lax.broadcasted_iota(jnp.int32, (slots, rows), 0) == slot_ref[...]
        ).astype(jnp.bfloat16)
        for t in range(steps):
            for g2 in range(4):
                y = jnp.dot(
                    onehot,
                    q_ref[t, :, g2 * 2 * HD : (g2 + 1) * 2 * HD],
                    preferred_element_type=jnp.float32,
                ).astype(jnp.bfloat16)
                for half in range(2):
                    tg = t * 8 + g2 * 2 + half
                    for m in range(PLANE):
                        for s in range(4):
                            base = (m * 4 + s) * cap
                            outs[m][0, s, tg * cap : (tg + 1) * cap, :] = y[
                                base : base + cap, half * HD : (half + 1) * HD
                            ]

    out = jax.ShapeDtypeStruct((per, 4, pairs * cap, HD), jnp.bfloat16)
    return pl.pallas_call(
        body,
        grid=(per,),
        in_specs=[
            pl.BlockSpec((1, rows), lambda k: (0, 0)),
            pl.BlockSpec((steps, rows, 8 * HD), lambda k: (0, 0, first + k)),
        ],
        out_specs=[pl.BlockSpec((1, 4, pairs * cap, HD), lambda k: (k, 0, 0, 0))] * PLANE,
        out_shape=[out] * PLANE,
        compiler_params=params(1),
        cost_estimate=pl.CostEstimate(
            flops=per * 2 * 256 * rows * 16 * HD, bytes_accessed=per * 3 << 19, transcendentals=0
        ),
        name="place_queries",
    )(slot_row, queries)


def pack_lse(lse, cap):
    pairs = lse.shape[0] // cap
    lse = lse.reshape(pairs, cap, HD)
    lane = lax.broadcasted_iota(jnp.int32, (cap, HD), 1)
    packed = jnp.zeros((cap, HD), jnp.float32)
    for tg in range(pairs):
        packed = jnp.where((lane & 15) == tg, lse[tg], packed)
    hi = packed.astype(jnp.bfloat16)
    rest = packed - hi.astype(jnp.float32)
    mid = rest.astype(jnp.bfloat16)
    low = (rest - mid.astype(jnp.float32)).astype(jnp.bfloat16)
    return jnp.where(lane < 16, hi, jnp.where(lane < 32, mid, low))


def prefix_tiles(count, read, keys, values, write):
    scores = dot_nt(read(0), keys)
    for i in range(count):
        ahead = dot_nt(read(i + 1), keys) if i + 1 < count else None
        highest = jnp.max(scores, axis=-1, keepdims=True)
        exp_terms = jnp.exp2(scores * EXP2_SCALE - highest * EXP2_SCALE)
        totals = jnp.sum(exp_terms, axis=-1, keepdims=True)
        summed = jnp.dot(
            exp_terms.astype(jnp.bfloat16), values, preferred_element_type=jnp.float32
        )
        part = (summed / totals).astype(jnp.bfloat16)
        lse = jnp.broadcast_to(highest * SCALE + jnp.log(totals), (scores.shape[0], HD))
        write(i, part, pack_lse(lse, 16))
        scores = ahead


def prefix_call(inner, sources, kvs, jobs, out_subs):
    flat = [a for group in sources for a in group]
    per, unit = sources[0][0].shape[0], sources[0][0].shape[2]
    cap = 16
    n_src, n_kv = len(flat), len(kvs)
    length = kvs[0].shape[1]
    places = []
    for group in sources:
        base = sum(len(g) for g in sources[: len(places)])
        places.append([(base + m, None) if len(group) == PLANE else (base, m) for m in range(PLANE)])

    def body(inner_ref, *refs):
        src = refs[:n_src]
        kv = refs[n_src : n_src + n_kv]
        outs = refs[n_src + n_kv :]
        job_id = pl.program_id(1)
        is_inner = inner_ref[0] == 1
        for ji, (si, sub, kv_inner, kv_end, oi, osub) in enumerate(jobs):

            def work(ki, si=si, sub=sub, oi=oi, osub=osub):
                def read(m):
                    ref, lead = places[si][m]
                    return src[ref][0, sub] if lead is None else src[ref][lead, 0, sub]

                def write(m, part, lse):
                    outs[oi * PLANE + m][0, osub, :unit] = part
                    outs[oi * PLANE + m][0, osub, unit:] = lse

                if ki is None:
                    for m in range(PLANE):
                        outs[oi * PLANE + m][0, osub] = jnp.zeros((unit + cap, HD), jnp.bfloat16)
                else:
                    prefix_tiles(PLANE, read, kv[ki][0], kv[ki][1], write)

            here = job_id == ji
            if kv_inner == kv_end:
                pl.when(here)(functools.partial(work, kv_inner))
            else:
                pl.when(jnp.logical_and(here, is_inner))(functools.partial(work, kv_inner))
                pl.when(jnp.logical_and(here, jnp.logical_not(is_inner)))(
                    functools.partial(work, kv_end)
                )

    def source_spec(a):
        if a.ndim == 4:
            return pl.BlockSpec((1,) + a.shape[1:], lambda k, j, inner: (k, 0, 0, 0))
        return pl.BlockSpec((PLANE, 1) + a.shape[2:], lambda k, j, inner: (0, k, 0, 0, 0))

    out_shape, out_specs = [], []
    for subs in out_subs:
        for _ in range(PLANE):
            out_shape.append(jax.ShapeDtypeStruct((per, subs, unit + cap, HD), jnp.bfloat16))
            out_specs.append(
                pl.BlockSpec((1, subs, unit + cap, HD), lambda k, j, inner: (k, 0, 0, 0))
            )
    work = per * len(jobs) * PLANE * unit * length
    outs = pl.pallas_call(
        body,
        grid_spec=pltpu.PrefetchScalarGridSpec(
            num_scalar_prefetch=1,
            grid=(per, len(jobs)),
            in_specs=[source_spec(a) for a in flat]
            + [pl.BlockSpec((2, length, HD), lambda k, j, inner: (0, 0, k)) for _ in kvs],
            out_specs=out_specs,
        ),
        out_shape=out_shape,
        compiler_params=params(2),
        cost_estimate=pl.CostEstimate(
            flops=work * 4 * HD * 2, bytes_accessed=per * 4 << 20, transcendentals=work
        ),
    )(inner, *flat, *kvs)
    return [list(outs[i * PLANE : (i + 1) * PLANE]) for i in range(len(out_subs))]


def gather_last(parts, *behind):
    per, subs, unit = parts[0].shape[:3]

    def body(*refs):
        for m in range(len(parts)):
            refs[-1][m] = refs[m][...]

    return pl.pallas_call(
        body,
        grid=(1,),
        in_specs=[pl.BlockSpec((per, 1, unit, HD), lambda i: (0, subs - 1, 0, 0)) for _ in parts]
        + [pl.BlockSpec(memory_space=pl.ANY)] * len(behind),
        out_specs=pl.BlockSpec((len(parts), per, 1, unit, HD), lambda i: (0, 0, 0, 0, 0)),
        out_shape=jax.ShapeDtypeStruct((len(parts), per, 1, unit, HD), jnp.bfloat16),
        compiler_params=params(1),
        name="gather_last",
    )(*parts, *behind)


def suffix_call(queries, new_kv, suffix_kv, key_row):
    steps, rows, width = queries.shape
    kv_heads = width // (8 * HD)
    cached = suffix_kv.shape[2]
    rb, blocks = 16, 4
    pairs = steps * 8
    keys_n = rb * cached
    span = rb * blocks

    def body(q_ref, new_ref, kv_ref, live_ref, acc_ref, stat_ref):
        row_id = lax.broadcasted_iota(jnp.int32, (pairs * rb, keys_n), 0) & (rb - 1)
        qi = lax.broadcasted_iota(jnp.int32, (pairs * rb, steps * rb), 0)
        ki = lax.broadcasted_iota(jnp.int32, (pairs * rb, steps * rb), 1)
        allowed = jnp.logical_and(
            (qi & (rb - 1)) == (ki & (rb - 1)), lax.div(ki, rb) <= lax.div(qi, 8 * rb)
        )
        lane = lax.broadcasted_iota(jnp.int32, (rb, HD), 1)

        def score(b):
            r = slice(b * rb, (b + 1) * rb)
            q = jnp.concatenate(
                [q_ref[t, r, g * HD : (g + 1) * HD] for t in range(steps) for g in range(8)],
                axis=0,
            )
            old = dot_nt(q, kv_ref[0, r].reshape(keys_n, HD))
            fresh = dot_nt(q, new_ref[0, :, r].reshape(steps * rb, HD))
            return old, fresh

        ahead = score(0)
        for b in range(blocks):
            old, fresh = ahead
            if b + 1 < blocks:
                ahead = score(b + 1)
            r = slice(b * rb, (b + 1) * rb)
            old = jnp.where(row_id == live_ref[b], old, NEG)
            fresh = jnp.where(allowed, fresh, NEG)
            highest = jnp.maximum(
                jnp.max(old, axis=-1, keepdims=True), jnp.max(fresh, axis=-1, keepdims=True)
            )
            exp_old = jnp.exp2((old - highest) * EXP2_SCALE)
            exp_fresh = jnp.exp2((fresh - highest) * EXP2_SCALE)
            totals = jnp.sum(exp_old, axis=-1, keepdims=True) + jnp.sum(
                exp_fresh, axis=-1, keepdims=True
            )
            acc = jnp.dot(
                exp_old.astype(jnp.bfloat16),
                kv_ref[1, r].reshape(keys_n, HD),
                preferred_element_type=jnp.float32,
            ) + jnp.dot(
                exp_fresh.astype(jnp.bfloat16),
                new_ref[1, :, r].reshape(steps * rb, HD),
                preferred_element_type=jnp.float32,
            )
            acc_ref[0, :, r] = acc.reshape(pairs, rb, HD)
            top = (highest * SCALE).reshape(pairs, rb, 1)
            totals = totals.reshape(pairs, rb, 1)
            stat = jnp.ones((rb, HD), jnp.float32)
            for tg in range(pairs):
                stat = jnp.where(lane == tg, top[tg], stat)
                stat = jnp.where(lane == pairs + tg, totals[tg], stat)
            stat_ref[0, r] = stat

    return pl.pallas_call(
        body,
        grid=(kv_heads, rows // span),
        in_specs=[
            pl.BlockSpec((steps, span, 8 * HD), lambda k, r: (0, r, k)),
            pl.BlockSpec((2, steps, span, HD), lambda k, r: (0, 0, r, k)),
            pl.BlockSpec((2, span, cached, HD), lambda k, r: (0, r, 0, k)),
            pl.BlockSpec((blocks, 1, keys_n), lambda k, r: (r, 0, 0)),
        ],
        out_specs=[
            pl.BlockSpec((1, pairs, span, HD), lambda k, r: (k, 0, r, 0)),
            pl.BlockSpec((1, span, HD), lambda k, r: (k, r, 0)),
        ],
        out_shape=[
            jax.ShapeDtypeStruct((kv_heads, pairs, rows, HD), jnp.float32),
            jax.ShapeDtypeStruct((kv_heads, rows, HD), jnp.float32),
        ],
        compiler_params=params(2),
        cost_estimate=pl.CostEstimate(
            flops=kv_heads * 8 * 256 * 512 * 512,
            bytes_accessed=16 << 20,
            transcendentals=kv_heads * 8 * 256 * 512,
        ),
        name="suffix_attention",
    )(queries, new_kv, suffix_kv, key_row)


def merge_call(spots, parts, suf_acc, suf_stat, first, per):
    unit = parts[0].shape[2] - 16
    cap = 16
    pairs = unit // cap
    rows = suf_acc.shape[2]
    places = [(i, s) for i, a in enumerate(parts) for s in range(a.shape[1])]
    total = len(places) * cap
    n = len(parts)

    def body(spot_ref, *refs):
        part = refs[:n]
        acc_ref, stat_ref, out_ref = refs[n:]
        onehot = (
            lax.broadcasted_iota(jnp.int32, (rows, total), 1) == spot_ref[...]
        ).astype(jnp.bfloat16)

        def column(lo):
            return jnp.concatenate([part[i][0, s, lo : lo + cap, :] for i, s in places], axis=0)

        def pick(block):
            return jnp.dot(onehot, block, preferred_element_type=jnp.float32)

        lse = pick(column(unit))
        lse = lse + pltpu.roll(lse, HD - 16, 1) + pltpu.roll(lse, HD - 32, 1)
        top = stat_ref[0]
        totals = pltpu.roll(top, HD - pairs, 1)
        joint = jnp.maximum(lse, top)
        pre = jnp.exp(lse - joint)
        suf = jnp.exp(top - joint)
        norm = pre + suf * totals
        pre = pre / norm
        suf = suf / norm
        for two in range(0, pairs, 2):
            both = pick(
                jnp.concatenate([column(two * cap), column((two + 1) * cap)], axis=1)
            )
            for tg in (two, two + 1):
                t, g = tg // 8, tg % 8
                mine = both[:, (tg - two) * HD : (tg - two + 1) * HD]
                mixed = pre[:, tg : tg + 1] * mine + suf[:, tg : tg + 1] * acc_ref[0, tg]
                out_ref[t * rows : (t + 1) * rows, g * HD : (g + 1) * HD] = mixed.astype(
                    jnp.bfloat16
                )

    return pl.pallas_call(
        body,
        grid=(per,),
        in_specs=[pl.BlockSpec((rows, 1), lambda k: (0, 0))]
        + [
            pl.BlockSpec((1,) + a.shape[1:], lambda k: (k, 0, 0, 0)) for a in parts
        ]
        + [
            pl.BlockSpec((1, pairs, rows, HD), lambda k: (first + k, 0, 0, 0)),
            pl.BlockSpec((1, rows, HD), lambda k: (first + k, 0, 0)),
        ],
        out_specs=pl.BlockSpec((2 * rows, 8 * HD), lambda k: (0, k)),
        out_shape=jax.ShapeDtypeStruct((2 * rows, per * 8 * HD), jnp.bfloat16),
        compiler_params=params(1, VMEM_PART),
        cost_estimate=pl.CostEstimate(
            flops=per * 17 * 2 * rows * total * HD, bytes_accessed=per * 4 << 20, transcendentals=0
        ),
        name="merge_parts",
    )(spots, *parts, suf_acc, suf_stat)


def project_call(half, attn, weight, prior, chunk, cols):
    rows, depth = attn.shape
    tile = 512
    steps = cols // tile

    def body(half_ref, attn_ref, w_ref, *refs):
        out = jnp.dot(attn_ref[...], w_ref[...], preferred_element_type=jnp.float32)
        if prior is not None:
            out = out + refs[0][...]
        refs[-1][...] = out

    in_specs = [
        pl.BlockSpec((rows, depth), lambda n, half: (0, 0)),
        pl.BlockSpec((depth, tile), lambda n, half: (chunk, half[0] * steps + n)),
    ]
    args = [attn, weight]
    if prior is not None:
        in_specs.append(pl.BlockSpec((rows, tile), lambda n, half: (0, half[0] * steps + n)))
        args.append(prior)
    return pl.pallas_call(
        body,
        grid_spec=pltpu.PrefetchScalarGridSpec(
            num_scalar_prefetch=1,
            grid=(steps,),
            in_specs=in_specs,
            out_specs=pl.BlockSpec((rows, tile), lambda n, half: (0, n)),
        ),
        out_shape=jax.ShapeDtypeStruct((rows, cols), jnp.float32),
        compiler_params=params(1, VMEM_PART),
        cost_estimate=pl.CostEstimate(
            flops=2 * rows * depth * cols,
            bytes_accessed=2 * depth * cols + 8 * rows * cols,
            transcendentals=0,
        ),
    )(half, *args)


def attend(query_slots, kv_blocks):
    count_n = query_slots.shape[0]
    count_c = query_slots.shape[1]
    kv_heads = kv_blocks.shape[-1] // HD
    group_size = query_slots.shape[-1] // (kv_heads * HD)
    query_grid = query_slots.reshape(count_n, count_c, 2, kv_heads, group_size, HD)
    key_grid = kv_blocks[:, 0].reshape(count_n, -1, kv_heads, HD)
    value_grid = kv_blocks[:, 1].reshape(count_n, -1, kv_heads, HD)
    scores = jnp.einsum(
        "nctkgd,npkd->nctkgp", query_grid, key_grid, preferred_element_type=jnp.float32
    ) * (1.0 / math.sqrt(HD))
    highest = jnp.max(scores, axis=-1)
    exp_terms = jnp.exp(scores - highest[..., None])
    totals = jnp.sum(exp_terms, axis=-1)
    prob_round = exp_terms.astype(jnp.bfloat16)
    summed = jnp.einsum(
        "nctkgp,npkd->nctkgd", prob_round, value_grid, preferred_element_type=jnp.float32
    )
    part_out = (summed / totals[..., None]).astype(jnp.bfloat16).reshape(count_n, count_c, 2, -1)
    part_lse = (highest + jnp.log(totals)).reshape(count_n, count_c, 2, -1)
    return (part_out, part_lse)


def merge_suffix(queries, new_kv, suffix_kv, suffix_len, pre_out, pre_lse):
    local_rows = queries.shape[1]
    kv_heads = suffix_kv.shape[-1] // HD
    group_size = queries.shape[-1] // (kv_heads * HD)
    cached = suffix_kv.shape[2]
    query_grid = jnp.transpose(queries, (1, 0, 2)).reshape(local_rows, 2, kv_heads, group_size, HD)
    new_rows = jnp.transpose(new_kv, (0, 2, 1, 3))
    key_grid = jnp.concatenate([suffix_kv[0], new_rows[0]], axis=1).reshape(
        local_rows, cached + 2, kv_heads, HD
    )
    value_grid = jnp.concatenate([suffix_kv[1], new_rows[1]], axis=1).reshape(
        local_rows, cached + 2, kv_heads, HD
    )
    scores = jnp.einsum(
        "rtkgd,rpkd->rtkgp", query_grid, key_grid, preferred_element_type=jnp.float32
    ) * (1.0 / math.sqrt(HD))
    position = jnp.arange(cached + 2, dtype=jnp.int32)[None, None, :]
    step_ids = jnp.arange(2, dtype=jnp.int32)[None, :, None]
    is_live = jnp.where(
        position < cached, position < suffix_len[:, None, None], position - cached <= step_ids
    )
    scores = jnp.where(is_live[:, :, None, None, :], scores, -jnp.inf)
    highest = jnp.max(scores, axis=-1)
    exp_terms = jnp.exp(scores - highest[..., None])
    totals = jnp.sum(exp_terms, axis=-1)
    prob_round = exp_terms.astype(jnp.bfloat16)
    summed = jnp.einsum(
        "rtkgp,rpkd->rtkgd", prob_round, value_grid, preferred_element_type=jnp.float32
    )
    prior_lse = pre_lse.reshape(local_rows, 2, kv_heads, group_size)
    prior_out = pre_out.astype(jnp.float32).reshape(local_rows, 2, kv_heads, group_size, HD)
    joint_top = jnp.maximum(prior_lse, highest)
    weight_pre = jnp.exp(prior_lse - joint_top)
    weight_suf = jnp.exp(highest - joint_top)
    mixed = (weight_pre[..., None] * prior_out + weight_suf[..., None] * summed) / (
        weight_pre + weight_suf * totals
    )[..., None]
    return mixed.astype(jnp.bfloat16).reshape(local_rows, 2, -1)


def gathered_device(
    queries, new_kv, suffix_kv, suffix_len, row_subtree, owner_rep, prefix_kv, out_weight
):
    local_rows = queries.shape[1]
    replicas = lax.axis_size("rep")
    capacity = 2 * local_rows // replicas
    subtrees = owner_rep.shape[0]
    sub_table = (row_subtree == jnp.arange(subtrees, dtype=jnp.int32)[None, :]).astype(jnp.int32)
    row_owner = jnp.sum(sub_table * owner_rep[None, :], axis=1)
    own_table = (row_owner[:, None] == jnp.arange(subtrees, dtype=jnp.int32)[None, :]).astype(
        jnp.int32
    )
    earlier = jnp.cumsum(own_table, axis=0) - own_table
    slot_index = row_owner * capacity + jnp.sum(earlier * own_table, axis=1)
    placing = (
        slot_index[None, :] == jnp.arange(subtrees * capacity, dtype=jnp.int32)[:, None]
    ).astype(jnp.bfloat16)
    query_slots = jnp.einsum(
        "sr,trx->stx", placing, queries, preferred_element_type=jnp.float32
    ).astype(jnp.bfloat16)
    query_slots = query_slots.reshape(subtrees, capacity, 2, -1)
    part_out, part_lse = attend(query_slots, lax.all_gather(prefix_kv, "rep", axis=0, tiled=True))
    pre_out = jnp.take(part_out.reshape(subtrees * capacity, 2, -1), slot_index, axis=0)
    pre_lse = jnp.take(part_lse.reshape(subtrees * capacity, 2, -1), slot_index, axis=0)
    attention = merge_suffix(queries, new_kv, suffix_kv, suffix_len, pre_out, pre_lse)
    attn_steps = jnp.transpose(attention, (1, 0, 2)).reshape(2 * local_rows, -1)
    head_terms = jnp.dot(attn_steps, out_weight, preferred_element_type=jnp.float32).reshape(
        2, local_rows, -1
    )
    return lax.psum_scatter(head_terms, "head", scatter_dimension=2, tiled=True).astype(
        jnp.bfloat16
    )


def routed_device(
    queries, new_kv, suffix_kv, suffix_len, row_subtree, owner_rep, prefix_kv, out_weight
):
    rows = queries.shape[1]
    replicas = lax.axis_size("rep")
    levels = replicas // PLANE
    me = lax.axis_index("rep")
    head = lax.axis_index("head")
    level, seat = me // PLANE, me % PLANE
    kv_heads = suffix_kv.shape[-1] // HD
    cached = suffix_kv.shape[2]
    cap = 16
    chunks, first = [], 0
    for share in SPLIT:
        per = int(share * kv_heads)
        chunks.append((first, per))
        first += per

    def perm(move):
        pairs = []
        for r in range(replicas):
            to = move(r // PLANE, r % PLANE)
            if to is not None:
                pairs.append((r, to[0] * PLANE + to[1]))
        return pairs

    def is_end(v):
        return v in (0, levels - 1)

    def send(a, move):
        return lax.ppermute(a, "rep", perm(move))

    def beside(m):
        return lambda v, s: (v, s ^ m)

    def to_pair(v, s):
        return (v ^ 1, s)

    def across(v, s):
        return None if is_end(v) else (levels - 1 - v, s)

    def inward(v, s):
        return (v ^ 1, s) if is_end(v) else None

    def outward(m):
        return lambda v, s: None if is_end(v) else (v ^ 1, s ^ m)

    def after(value, *others):
        return lax.optimization_barrier((value,) + others)[0]

    sub_table = row_subtree == jnp.arange(owner_rep.shape[0], dtype=jnp.int32)[None, :]
    owner = jnp.sum(jnp.where(sub_table, owner_rep[None, :], 0), axis=1)
    ids = jnp.arange(rows, dtype=jnp.int32)
    rank = jnp.sum(
        jnp.logical_and(owner[:, None] == owner[None, :], ids[None, :] < ids[:, None]).astype(
            jnp.int32
        ),
        axis=1,
    )
    owner_level, owner_seat = owner // PLANE, owner % PLANE
    partner = owner_seat ^ seat
    end_level = jnp.logical_or(owner_level == 0, owner_level == levels - 1)
    kind = jnp.where(
        owner_level == level,
        0,
        jnp.where(owner_level == (level ^ 1), 1, jnp.where(end_level, 3, 2)),
    )
    slot = (partner * 4 + kind) * cap + rank
    inner = jnp.logical_not(jnp.logical_or(level == 0, level == levels - 1))
    base = PLANE * 2 * cap
    spots = jnp.where(
        kind < 2,
        (partner * 2 + kind) * cap,
        jnp.where(
            jnp.logical_or(kind == 2, inner),
            base + (partner * 2 + kind - 2) * cap,
            2 * base + partner * cap,
        ),
    )
    spots = (spots + rank)[:, None]
    inner_flag = inner.astype(jnp.int32)[None]
    position = jnp.arange(cached, dtype=jnp.int32)[None, :]
    key_row = jnp.where(position < suffix_len[:, None], (ids & 15)[:, None], -1).reshape(
        rows // 16, 1, 16 * cached
    )

    own, pair, mid, asked = [], [], [], []
    source = prefix_kv
    for first, per in chunks:
        kv = source[0, :, :, first * HD : (first + per) * HD]
        own.append(kv)
        pair.append(send(kv, to_pair))
        mid.append(send(kv, across))
        mine = place_queries(slot[None, :], queries, first, per)
        asked.append([mine[0]] + [send(mine[m], beside(m)) for m in range(1, PLANE)])
        source = after(prefix_kv, mine[0])

    suf_acc, suf_stat = suffix_call(queries, new_kv, suffix_kv, after(key_row, mine[0]))

    far, mid_end, asked_ends, near = [], [], [], []
    for c, (first, per) in enumerate(chunks):
        far.append(send(pair[c], across))
        mid_end.append(send(mid[c], outward(0)))
        asked_ends.append(send(gather_last(asked[c], *[n[0] for n in near]), inward))
        (found,) = prefix_call(
            inner_flag, [asked[c]], [own[c], pair[c]], [(0, 0, 0, 0, 0, 0), (0, 1, 1, 1, 0, 1)], [2]
        )
        near.append([found[0]] + [send(found[m], beside(m)) for m in range(1, PLANE)])

    rest = []
    for c in range(len(chunks)):
        here, ends = prefix_call(
            inner_flag,
            [asked[c], [asked_ends[c]]],
            [mid[c], mid_end[c], far[c]],
            [(1, 0, 2, None, 1, 0), (0, 2, 0, 1, 0, 0), (0, 3, 2, None, 0, 1)],
            [2, 1],
        )
        ends = [send(ends[m], outward(m)) for m in range(PLANE)]
        here = [here[0]] + [send(here[m], beside(m)) for m in range(1, PLANE)]
        rest.append(here + ends)

    total = None
    zero = jnp.zeros((1,), jnp.int32)
    for c, (first, per) in enumerate(chunks):
        attn = merge_call(spots, near[c] + rest[c], suf_acc, suf_stat, first, per)
        block = first // per
        if c < len(chunks) - 1:
            total = project_call(zero, attn, out_weight, total, block, out_weight.shape[1])
    half = out_weight.shape[1] // 2
    theirs = project_call((1 - head).astype(jnp.int32)[None], attn, out_weight, total, block, half)
    theirs = lax.ppermute(theirs, "head", [(0, 1), (1, 0)])
    ours = project_call(head.astype(jnp.int32)[None], attn, out_weight, total, block, half)
    return (ours + theirs).astype(jnp.bfloat16).reshape(2, rows, half)


def solution(mesh):
    placed = (
        P(None, "rep", "head"),
        P(None, None, "rep", "head"),
        P(None, "rep", None, "head"),
        P("rep"),
        P("rep", None),
        P(),
        P("rep", None, None, "head"),
        P("head", None),
    )

    def routed(*args):
        return routed_device(*args)

    line_of_four = mesh.shape["rep"] == 4 * PLANE and mesh.shape["head"] == 2
    return jax.shard_map(
        routed if line_of_four else gathered_device,
        mesh=mesh,
        in_specs=placed,
        out_specs=P(None, "rep", "head"),
        check_vma=False,
    )
```
